32 devices in a mesh: rows: 16 (over z, y, x), rep: 2 (over core).
Axes of the slice: x: 2, y: 2, z: 4, core: 2. Of those that a mesh axis runs over, the one named last changes fastest.
Arguments:
- features: bfloat16 [4096, 128], P(('rows', 'rep')), may hold values from -6 to 6
- tile_counts: int32 [4096, 128, 128], P(('rows', 'rep')), may hold values from 0 to 3, as said below
- tile_row: int32 [4096], P(('rows', 'rep')), may hold values from 0 to 1
- tile_col: int32 [4096], P(('rows', 'rep')), may hold values from 0 to 31, as said below
- label_ids: int32 [2048], P(('rows', 'rep')), may hold values from 0 to 4095, as said below
- cotangent: bfloat16 [4096, 256], P(('rows', 'rep')), may hold values from -6 to 6
- self_weight: bfloat16 [128, 256], replicated, may hold values from -0.5 to 0.5
- neigh_weight: bfloat16 [128, 256], replicated, may hold values from -0.5 to 0.5
Outputs:
- activation: bfloat16 [4096, 256], P(('rows', 'rep'))
- grad_features: float32 [4096, 128], P(('rows', 'rep'))
- grad_self: float32 [128, 256], replicated
- grad_neigh: float32 [128, 256], replicated
The draws below stay inside these ranges and needn't reach their ends.
Inputs may be any that keep to these rules, and one draw needn't show every extreme that they name: `tile_counts`: edge counts of one tile; most entries are zero. `tile_col`: every tile held by a device of rep index c names a column block of the feature rows of some device of rep index c. On each device, at most 16 tiles name column blocks held by devices of one rows index, and exactly 16 do for some rows index. `label_ids`: the ids of one device's 64 labels are distinct and lie among that device's own feature rows.
All inputs are finite; a program needn't handle non-finite values.
Results may differ from the reference program's by a relative error of at most 0.0053.
Values may be sent and summed in bfloat16 or wider, within the bound.
A program may use at most 128 MiB of HBM per device.

```python
import jax
import jax.numpy as jnp
from jax import lax

F_IN = 128
HID = 256
BLOCK = 128
NODES_DEV = 256
TILE_DEV = 128
HALF = 128
CAP = 16
LAB_DEV = 64
NODES = 4096
TILES = 4096
LABELS = 2048
N_ROWS = 16
N_REP = 2


def draw_tile_counts(key, part):
    present = jax.random.randint(key, (TILES, BLOCK, BLOCK), 0, 32, dtype=jnp.int32) == 0
    values = jax.random.randint(jax.random.fold_in(key, 1), (TILES, BLOCK, BLOCK), 1, 4, dtype=jnp.int32)
    return jnp.where(present, values, 0).astype(jnp.int32)


def draw_tile_col(key, part):
    per_half = HALF // BLOCK
    slot_total = CAP * N_ROWS

    def single(which):
        device_key = jax.random.fold_in(key, which)
        replica = which % N_REP
        owner_order = jax.random.permutation(jax.random.fold_in(device_key, 1), N_ROWS).astype(jnp.int32)
        slot_owner = owner_order[jnp.arange(slot_total, dtype=jnp.int32) // CAP]
        rest = jax.random.permutation(jax.random.fold_in(device_key, 2), slot_total - CAP).astype(jnp.int32)[:TILE_DEV - CAP] + CAP
        chosen = jnp.concatenate([jnp.arange(CAP, dtype=jnp.int32), rest])
        owners = slot_owner[chosen]
        shuffle = jax.random.permutation(jax.random.fold_in(device_key, 3), TILE_DEV).astype(jnp.int32)
        owners = owners[shuffle]
        within = jax.random.randint(jax.random.fold_in(device_key, 4), (TILE_DEV,), 0, per_half, dtype=jnp.int32)
        return ((owners * N_REP + replica) * per_half + within).astype(jnp.int32)
    return jax.vmap(single)(jnp.arange(N_ROWS * N_REP, dtype=jnp.int32)).reshape(-1).astype(jnp.int32)


def draw_label_ids(key, part):

    def single(which):
        shuffled = jax.random.permutation(jax.random.fold_in(key, which), HALF)
        return shuffled[:LAB_DEV].astype(jnp.int32) + which * HALF
    return jax.vmap(single)(jnp.arange(N_ROWS * N_REP, dtype=jnp.int32)).reshape(-1).astype(jnp.int32)


def place_ends(array, own_key, least, largest):
    spot = [jax.random.randint(jax.random.fold_in(own_key, axis), (), 0, length) for axis, length in enumerate(array.shape)]
    main_axis = array.shape.index(max(array.shape))
    beside = spot[:main_axis] + [(spot[main_axis] + 1) % array.shape[main_axis]] + spot[main_axis + 1:]
    return array.at[tuple(spot)].set(least).at[tuple(beside)].set(largest)


def levels(key, dims, split, smallest, largest):
    loudness, own = 1.0, jax.random.fold_in(key, 6)
    for position, blocks in split:
        draws = jnp.exp(jax.random.uniform(jax.random.fold_in(own, position), (blocks,), jnp.float32, smallest / len(split), largest / len(split)))
        loudness = loudness * jnp.repeat(draws, dims[position] // blocks).reshape([-1 if axis == position else 1 for axis in range(len(dims))])
    return loudness


def scatter_about(own_key, extent, scale, most, cuts=(), kind=jnp.bfloat16):
    array = scale * jax.random.normal(own_key, extent, jnp.float32)
    if cuts:
        array = array * levels(own_key, extent, cuts, -0.22, 0.18)
    return jnp.clip(array, -most, most).astype(kind)


def setup_inputs(seed: int = 0) -> dict:
    seeds = jax.random.split(jax.random.key(seed), 9)
    return {
        "features": scatter_about(seeds[0], (NODES, F_IN), 1.0, 6.0, ((0, 32),)),
        "tile_counts": draw_tile_counts(jax.random.fold_in(seeds[8], 71), 0),
        "tile_row": place_ends(jax.random.randint(seeds[2], (TILES,), 0, NODES_DEV // BLOCK), jax.random.fold_in(seeds[2], 1), 0, (NODES_DEV // BLOCK) - 1).astype(jnp.int32),
        "tile_col": draw_tile_col(jax.random.fold_in(seeds[8], 71), 0),
        "label_ids": draw_label_ids(jax.random.fold_in(seeds[8], 71), 0),
        "cotangent": scatter_about(seeds[5], (NODES, HID), 1.0, 6.0, ((0, 32),)),
        "self_weight": scatter_about(seeds[6], (F_IN, HID), F_IN ** -0.5, 0.5),
        "neigh_weight": scatter_about(seeds[7], (F_IN, HID), F_IN ** -0.5, 0.5),
    }


edge_moment = 14.0 / 96.0


def reference(features, tile_counts, tile_row, tile_col, label_ids, cotangent, self_weight, neigh_weight):
    row_blocks = NODES_DEV // BLOCK
    scale = (edge_moment * TILE_DEV * N_REP * BLOCK / row_blocks) ** -0.5
    group_tiles = TILE_DEV * N_REP
    counts = tile_counts.reshape(N_ROWS, group_tiles, BLOCK, BLOCK)
    rows_of = tile_row.reshape(N_ROWS, group_tiles)
    cols_of = tile_col.reshape(N_ROWS, group_tiles)
    feature_blocks = features.reshape(NODES // BLOCK, BLOCK, F_IN)

    def gather_group(inputs):
        count_part, row_part, col_part = inputs
        panels = feature_blocks[col_part].astype(jnp.float32)
        products = jnp.einsum('tij,tjf->tif', count_part.astype(jnp.float32), panels, precision=lax.Precision.HIGHEST)
        owner_table = (row_part[:, None] == jnp.arange(row_blocks, dtype=jnp.int32)[None, :]).astype(jnp.float32)
        return jnp.einsum('tr,tif->rif', owner_table, products, precision=lax.Precision.HIGHEST)

    summed = lax.map(gather_group, (counts, rows_of, cols_of)).reshape(NODES, F_IN)
    neighbour = (scale * summed).astype(jnp.bfloat16)
    preact = jnp.dot(features, self_weight, preferred_element_type=jnp.float32) + jnp.dot(neighbour, neigh_weight, preferred_element_type=jnp.float32)
    activation = jax.nn.silu(preact).astype(jnp.bfloat16)
    label_mask = jnp.zeros((NODES,), jnp.float32).at[label_ids].set(1.0)
    masked = cotangent.astype(jnp.float32) * label_mask[:, None]
    sigma = jax.nn.sigmoid(preact)
    delta = (masked * sigma * (1.0 + preact * (1.0 - sigma))).astype(jnp.bfloat16)
    grad_scale = float(LABELS) ** -0.5
    grad_self = grad_scale * jnp.einsum('nf,nh->fh', features.astype(jnp.float32), delta.astype(jnp.float32), precision=lax.Precision.HIGHEST)
    grad_neigh = grad_scale * jnp.einsum('nf,nh->fh', neighbour.astype(jnp.float32), delta.astype(jnp.float32), precision=lax.Precision.HIGHEST)
    back = jnp.einsum('nh,fh->nf', delta.astype(jnp.float32), neigh_weight.astype(jnp.float32), precision=lax.Precision.HIGHEST).astype(jnp.bfloat16)
    back_blocks = back.reshape(N_ROWS, row_blocks, BLOCK, F_IN)

    def spread(total, inputs):
        count_part, row_part, col_part, back_part = inputs
        picked = back_part[row_part].astype(jnp.float32)
        terms = jnp.einsum('tij,tif->tjf', count_part.astype(jnp.float32), picked, precision=lax.Precision.HIGHEST)
        rounded = lax.optimization_barrier(terms.astype(jnp.bfloat16))
        return total.at[col_part].add(rounded.astype(jnp.float32)), None

    start_total = jnp.zeros((NODES // BLOCK, BLOCK, F_IN), jnp.float32)
    total, unused = lax.scan(spread, start_total, (counts, rows_of, cols_of, back_blocks))
    own_term = jnp.einsum('nh,fh->nf', delta.astype(jnp.float32), self_weight.astype(jnp.float32), precision=lax.Precision.HIGHEST)
    grad_features = own_term + scale * total.reshape(NODES, F_IN)
    return (activation, grad_features, grad_self, grad_neigh)
```

```python
import functools

import jax
import jax.numpy as jnp
from jax import lax
from jax.experimental import pallas as pl
from jax.experimental.pallas import tpu as pltpu
from jax.sharding import PartitionSpec as P

edge_moment = 14.0 / 96.0
MESH = pl.DeviceIdType.MESH
NT = (((1,), (1,)), ((), ()))
TN = (((0,), (0,)), ((), ()))


def dot(a, b, dims=(((1,), (0,)), ((), ()))):
    return lax.dot_general(a, b, dims, preferred_element_type=jnp.float32)


def finish_kernel(*refs):
    count = len(refs) // 2
    sems = refs[-1]
    copies = [
        pltpu.make_async_copy(refs[k], refs[count + k], sems.at[k]) for k in range(count)
    ]
    for copy in copies:
        copy.start()
    for copy in copies:
        copy.wait()


def finish(arrays):
    return pl.pallas_call(
        finish_kernel,
        out_shape=tuple(jax.ShapeDtypeStruct(a.shape, a.dtype) for a in arrays),
        in_specs=[pl.BlockSpec(memory_space=pltpu.VMEM)] * len(arrays),
        out_specs=tuple(pl.BlockSpec(memory_space=pl.ANY) for _ in arrays),
        scratch_shapes=[pltpu.SemaphoreType.DMA((len(arrays),))],
        compiler_params=pltpu.CompilerParams(vmem_limit_bytes=4 * 1024 * 1024),
        name="finish",
    )(*arrays)


def layer_kernel(
    n, zs, ps, scale, grad_scale,
    rows_h, cols_h, counts, feat_h, ids_h, cot_h, ws_h, wn_h,
    act_out, grad_out, self_out, neigh_out,
    rows_v, cols_v, feat, ids, cot, ws, wn, pick, buf, adj, gath, part, part_in, bt, tt, r1, s2, r2, wpart, win, wc, wr1, wz, wo,
    ag_s, ag_r, pair_s, pair_r, r1_s, r1_r, r2_s, r2_r, w1_s, w1_r, wz_s, wz_r, wo_s, wo_r, tile_s, in_s,
):
    me = lax.axis_index("rows")
    rep = lax.axis_index("rep")
    other = 1 - rep
    mz, mp = me // ps, me % ps
    half, f_in = feat.shape

    def zrow(d):
        return (mz + d) % zs

    def prow(d):
        return (mp + d) % ps

    def send(src, dst, ssem, rsem, row, core):
        copy = pltpu.make_async_remote_copy(
            src_ref=src, dst_ref=dst, send_sem=ssem, recv_sem=rsem,
            device_id=(row, core), device_id_type=MESH,
        )
        copy.start()
        sent.append(copy)
        return copy

    def arrived(dst, ssem, rsem):
        pltpu.make_async_remote_copy(
            src_ref=dst, dst_ref=dst, send_sem=ssem, recv_sem=rsem,
            device_id=(me, other), device_id_type=MESH,
        ).wait_recv()

    sent = []
    tiles = counts.shape[0]
    parts = tile_s.shape[0]
    size = half // parts
    loads = []
    for k, (src, dst) in enumerate((
        (feat_h, feat), (rows_h, rows_v), (cols_h, cols_v), (ids_h, ids), (cot_h, cot),
        (ws_h, ws), (wn_h, wn),
    )):
        loads.append(pltpu.make_async_copy(src, dst, in_s.at[k]))
        loads[-1].start()

    def part_copy(c):
        span_i = pl.ds(pl.multiple_of(c * size, size), size)
        return pltpu.make_async_copy(counts.at[:, span_i], buf.at[:, span_i], tile_s.at[c])

    for c in range(parts):
        part_copy(c).start()
    barrier = pltpu.get_barrier_semaphore()
    for d in range(1, zs):
        pl.semaphore_signal(barrier, inc=1, device_id=(zrow(d) * ps + mp, rep), device_id_type=MESH)
    for d in range(1, ps):
        for core in (rep, other):
            pl.semaphore_signal(
                barrier, inc=1, device_id=(mz * ps + prow(d), core), device_id_type=MESH
            )
    pl.semaphore_signal(barrier, inc=1, device_id=(me, other), device_id_type=MESH)
    pl.semaphore_wait(barrier, zs + 2 * (ps - 1))

    loads[0].wait()
    for d in range(1, zs):
        send(feat, gath.at[me], ag_s.at[d - 1], ag_r.at[me], zrow(d) * ps + mp, rep)
    for d in range(1, ps):
        send(feat, gath.at[me], ag_s.at[zs - 2 + d], ag_r.at[me], mz * ps + prow(d), rep)
    for load in loads[1:]:
        load.wait()

    wide = pick.shape[1]
    sub = wide // tiles
    lane = lax.broadcasted_iota(jnp.int32, (tiles, wide), 1)
    widen = (lane // sub == lax.broadcasted_iota(jnp.int32, (tiles, wide), 0)).astype(jnp.float32)
    both = jnp.concatenate(
        [
            jnp.broadcast_to(rows_v[...], (8, tiles)),
            jnp.broadcast_to(cols_v[...] // 2, (8, tiles)),
        ],
        axis=0,
    ).astype(jnp.float32).astype(jnp.bfloat16)
    spread = dot(both, widen.astype(jnp.bfloat16)).astype(jnp.int32)
    place = (spread[:1] * n + spread[8:9]) * sub + lane[:1] % sub
    chunk = min(pick.shape[0], 2 * half)

    def pick_rows(b):
        at = lax.broadcasted_iota(jnp.int32, (chunk, wide), 0) + b * chunk
        pick[pl.ds(b * chunk, chunk), :] = (at == place).astype(jnp.float32).astype(jnp.bfloat16)

    def build(g):
        lows, highs = [
            buf[:, pl.ds(pl.multiple_of(g * size + k * sub, sub), sub), :]
            .astype(jnp.float32).reshape(wide, half).astype(jnp.bfloat16)
            for k in range(2)
        ]
        rhs = jnp.concatenate([lows, highs], axis=1)

        def fill(b):
            out = dot(pick[pl.ds(b * chunk, chunk), :], rhs)
            for k in range(chunk // sub):
                cell = b * (chunk // sub) + k
                pair = out[k * sub : (k + 1) * sub]
                adj[
                    pl.ds(pl.multiple_of(cell // n * half + g * size, size), size),
                    pl.ds(pl.multiple_of(cell % n * half, half), half),
                ] = jnp.concatenate([pair[:, :half], pair[:, half:]], axis=0).astype(jnp.bfloat16)

        blocks = pick.shape[0] // chunk
        if blocks == 1:
            fill(0)
        else:
            pl.loop(0, blocks)(fill)

    for b in range(pick.shape[0] // chunk):
        pick_rows(b)
    gath[me] = feat[...]
    first = dot(feat[...], ws[...])
    near = lax.broadcasted_iota(jnp.int32, (half, ids.shape[1]), 0)
    hits = (near == ids[...] - (me * 2 + rep) * half).astype(jnp.float32)
    masked = cot[...].astype(jnp.float32) * jnp.max(hits, axis=1, keepdims=True)

    def pass_on(e):
        src = zrow(zs - e) * ps + mp
        arrived(gath.at[src], ag_s.at[0], ag_r.at[src])
        for d in range(1, ps):
            send(
                gath.at[src], gath.at[src], ag_s.at[zs - 2 + e * (ps - 1) + d], ag_r.at[src],
                mz * ps + prow(d), rep,
            )

    @pl.loop(0, parts)
    def _(g):
        part_copy(g).wait()
        build(g)

    for e in range(1, zs):
        pass_on(e)

    span = ps * half

    def plane_cols(zt):
        return adj[:, pl.ds(pl.multiple_of(zt * span, span), span)]

    total = jnp.zeros((2 * half, f_in), jnp.float32)
    for e in range(zs):
        zt = zrow(zs - e)
        for d in range(1, ps):
            src = zt * ps + prow(ps - d)
            arrived(gath.at[src], ag_s.at[0], ag_r.at[src])
        total = total + dot(plane_cols(zt), gath[pl.ds(zt * ps, ps)].reshape(span, f_in))
    part[...] = total.reshape(2, half, f_in)
    send(part.at[other], part_in, pair_s.at[0], pair_r.at[0], me, other)
    arrived(part_in, pair_s.at[0], pair_r.at[0])
    neighbour = (scale * (part[rep] + part_in[...])).astype(jnp.bfloat16)
    preact = first + dot(neighbour, wn[...])
    sigma = jax.nn.sigmoid(preact)
    act_out[...] = (preact * sigma).astype(jnp.bfloat16)
    delta = (masked * sigma * (1.0 + preact * (1.0 - sigma))).astype(jnp.bfloat16)
    bt[rep] = dot(wn[...], delta, NT).astype(jnp.bfloat16)
    send(bt.at[rep], bt.at[rep], pair_s.at[1], pair_r.at[1], me, other)
    wpart[0] = dot(feat[...], delta, TN)
    wpart[1] = dot(neighbour, delta, TN)
    send(wpart.at[other], win, pair_s.at[2], pair_r.at[2], me, other)
    own_term = dot(delta, ws[...], NT)

    arrived(bt.at[other], pair_s.at[1], pair_r.at[1])
    back = jnp.concatenate([bt[0], bt[1]], axis=1)

    def products(e):
        zt = zrow(e)
        out = dot(back, plane_cols(zt))
        for j in range(ps):
            tt[zt * ps + j] = out[:, j * half : (j + 1) * half].astype(jnp.bfloat16)
        for d in range(1, ps):
            k = zt * (ps - 1) + d - 1
            send(
                tt.at[zt * ps + prow(d)], r1.at[k], r1_s.at[(e - 1) * (ps - 1) + d - 1],
                r1_r.at[k], mz * ps + prow(d), rep,
            )

    products(1)
    arrived(win, pair_s.at[2], pair_r.at[2])
    wc[...] = (wpart[rep] + win[...]).astype(jnp.bfloat16).reshape(wc.shape)
    for d in range(1, ps):
        send(
            wc.at[prow(d)], wr1.at[d - 1], w1_s.at[d - 1], w1_r.at[d - 1], mz * ps + prow(d), rep
        )
    for e in range(2, zs + 1):
        products(e)
    shard = wc[mp].astype(jnp.float32)
    for d in range(1, ps):
        arrived(wr1.at[d - 1], w1_s.at[0], w1_r.at[d - 1])
        shard = shard + wr1[d - 1].astype(jnp.float32)
    wz[mz] = shard.astype(jnp.bfloat16)
    for d in range(1, zs):
        send(wz.at[mz], wz.at[mz], wz_s.at[d - 1], wz_r.at[mz], zrow(d) * ps + mp, rep)

    def plane_sum(zt):
        total = tt[zt * ps + mp].astype(jnp.float32)
        for d in range(1, ps):
            k = zt * (ps - 1) + d - 1
            arrived(r1.at[k], r1_s.at[0], r1_r.at[k])
            total = total + r1[k].astype(jnp.float32)
        return total

    for e in range(1, zs):
        s2[e - 1] = plane_sum(zrow(e)).astype(jnp.bfloat16)
        send(s2.at[e - 1], r2.at[e - 1], r2_s.at[e - 1], r2_r.at[e - 1], zrow(e) * ps + mp, rep)
    for d in range(1, zs):
        src = zrow(d)
        arrived(wz.at[src], wz_s.at[0], wz_r.at[src])
    shard = wz[0].astype(jnp.float32)
    for k in range(1, zs):
        shard = shard + wz[k].astype(jnp.float32)
    wo[rep, mp] = (grad_scale * shard).astype(jnp.bfloat16)
    send(wo.at[rep, mp], wo.at[rep, mp], wo_s.at[0], wo_r.at[rep, mp], me, other)
    for d in range(1, ps):
        for c, core in enumerate((rep, other)):
            send(
                wo.at[rep, mp], wo.at[rep, mp], wo_s.at[2 * d - 1 + c], wo_r.at[rep, mp],
                mz * ps + prow(d), core,
            )
    total = plane_sum(mz)
    for e in range(1, zs):
        arrived(r2.at[e - 1], r2_s.at[0], r2_r.at[e - 1])
        total = total + r2[e - 1].astype(jnp.float32)
    grad_out[...] = own_term + scale * jnp.transpose(total)
    arrived(wo.at[other, mp], wo_s.at[0], wo_r.at[other, mp])
    for d in range(1, ps):
        src = prow(d)
        for core in (rep, other):
            arrived(wo.at[core, src], wo_s.at[0], wo_r.at[core, src])
    self_out[...] = wo[0].astype(jnp.float32).reshape(self_out.shape)
    neigh_out[...] = wo[1].astype(jnp.float32).reshape(neigh_out.shape)
    for copy in sent:
        copy.wait_send()


def plane_size(n, width):
    return max(d for d in range(1, n + 1) if n % d == 0 and d * d <= 2 * n and width % (8 * d) == 0)


def shards(
    features, tile_counts, tile_row, tile_col, label_ids, cotangent, self_weight, neigh_weight
):
    half, f_in = features.shape
    hid = cotangent.shape[1]
    tile_total, block, _ = tile_counts.shape
    rep_count = lax.axis_size("rep")
    n = lax.axis_size("rows")
    per_half = half // block
    row_blocks = rep_count * per_half
    scale = (edge_moment * tile_total * rep_count * block / row_blocks) ** (-0.5)
    grad_scale = float(label_ids.shape[0] * n * rep_count) ** (-0.5)
    parts = half // 16
    sub = 8
    ps = plane_size(n, f_in)
    zs = n // ps
    bf, f4 = jnp.bfloat16, jnp.float32
    dma = pltpu.SemaphoreType.DMA
    vmem = pl.BlockSpec(memory_space=pltpu.VMEM)
    outs = pl.pallas_call(
        functools.partial(layer_kernel, n, zs, ps, scale, grad_scale),
        out_shape=(
            jax.ShapeDtypeStruct((half, hid), bf),
            jax.ShapeDtypeStruct((half, f_in), f4),
            jax.ShapeDtypeStruct((f_in, hid), f4),
            jax.ShapeDtypeStruct((f_in, hid), f4),
        ),
        in_specs=[pl.BlockSpec(memory_space=pltpu.HBM)] * 8,
        out_specs=(vmem,) * 4,
        scratch_shapes=[
            pltpu.VMEM((1, tile_total), jnp.int32),
            pltpu.VMEM((1, tile_total), jnp.int32),
            pltpu.VMEM((half, f_in), bf),
            pltpu.VMEM((1, label_ids.shape[0]), jnp.int32),
            pltpu.VMEM((half, hid), bf),
            pltpu.VMEM((f_in, hid), bf),
            pltpu.VMEM((f_in, hid), bf),
            pltpu.VMEM((row_blocks * n * sub, tile_total * sub), bf),
            pltpu.VMEM((tile_total, block, block), jnp.int32),
            pltpu.VMEM((row_blocks * block, n * block), bf),
            pltpu.VMEM((n, half, f_in), bf),
            pltpu.VMEM((2, half, f_in), f4),
            pltpu.VMEM((half, f_in), f4),
            pltpu.VMEM((2, f_in, half), bf),
            pltpu.VMEM((n, f_in, half), bf),
            pltpu.VMEM((zs * (ps - 1), f_in, half), bf),
            pltpu.VMEM((zs - 1, f_in, half), bf),
            pltpu.VMEM((zs - 1, f_in, half), bf),
            pltpu.VMEM((2, f_in, hid), f4),
            pltpu.VMEM((f_in, hid), f4),
            pltpu.VMEM((ps, f_in // ps, hid), bf),
            pltpu.VMEM((ps - 1, f_in // ps, hid), bf),
            pltpu.VMEM((zs, f_in // ps, hid), bf),
            pltpu.VMEM((2, ps, f_in // ps, hid), bf),
            dma((n,)), dma((n,)), dma((3,)), dma((3,)),
            dma((zs * (ps - 1),)), dma((zs * (ps - 1),)), dma((zs - 1,)), dma((zs - 1,)),
            dma((ps - 1,)), dma((ps - 1,)), dma((zs - 1,)), dma((zs,)),
            dma((2 * ps - 1,)), dma((2, ps)), dma((parts,)), dma((7,)),
        ],
        compiler_params=pltpu.CompilerParams(
            collective_id=0, has_side_effects=True, vmem_limit_bytes=50 * 1024 * 1024
        ),
        name="layer",
    )(*[
        pltpu.with_memory_space_constraint(a, pltpu.HBM)
        for a in (
            tile_row.reshape(1, -1), tile_col.reshape(1, -1), tile_counts, features,
            label_ids.reshape(1, -1), cotangent, self_weight, neigh_weight,
        )
    ])
    return finish(outs)


def solution(mesh):
    placed = (
        P(("rows", "rep"), None),
        P(("rows", "rep"), None, None),
        P(("rows", "rep")),
        P(("rows", "rep")),
        P(("rows", "rep")),
        P(("rows", "rep"), None),
        P(),
        P(),
    )
    return jax.shard_map(
        shards,
        mesh=mesh,
        in_specs=placed,
        out_specs=(P(("rows", "rep"), None), P(("rows", "rep"), None), P(), P()),
        check_vma=False,
    )
```

```python
import functools

import jax
import jax.numpy as jnp
from jax import lax
from jax.experimental import pallas as pl
from jax.experimental.pallas import tpu as pltpu
from jax.sharding import PartitionSpec as P

edge_moment = 14.0 / 96.0
MESH = pl.DeviceIdType.MESH
NT = (((1,), (1,)), ((), ()))
TN = (((0,), (0,)), ((), ()))


def dot(a, b, dims=(((1,), (0,)), ((), ()))):
    return lax.dot_general(a, b, dims, preferred_element_type=jnp.float32)


def finish_kernel(*refs):
    count = len(refs) // 2
    sems = refs[-1]
    copies = [
        pltpu.make_async_copy(refs[k], refs[count + k], sems.at[k]) for k in range(count)
    ]
    for copy in copies:
        copy.start()
    for copy in copies:
        copy.wait()


def finish(arrays):
    return pl.pallas_call(
        finish_kernel,
        out_shape=tuple(jax.ShapeDtypeStruct(a.shape, a.dtype) for a in arrays),
        in_specs=[pl.BlockSpec(memory_space=pltpu.VMEM)] * len(arrays),
        out_specs=tuple(pl.BlockSpec(memory_space=pl.ANY) for _ in arrays),
        scratch_shapes=[pltpu.SemaphoreType.DMA((len(arrays),))],
        compiler_params=pltpu.CompilerParams(vmem_limit_bytes=4 * 1024 * 1024),
        name="finish",
    )(*arrays)


def flip(a, k):
    out, bit = a, 1
    while bit <= k:
        if k & bit:
            out = out + (1 - 2 * ((a // bit) % 2)) * bit
        bit *= 2
    return out


def layer_kernel(
    n, zs, ps, scale, grad_scale,
    rows_h, cols_h, counts, feat_h, ids_h, cot_h, ws_h, wn_h,
    act_out, grad_out, self_out, neigh_out,
    rows_v, cols_v, feat, ids, cot, ws, wn, pick, buf, adj, gath, part, part_in, bt, tt, r1, s2, r2, wpart, win, wz, wo,
    ag_s, ag_r, pair_s, pair_r, r1_s, r1_r, r2_s, r2_r, w1_s, w1_r, wz_s, wz_r, wo_s, wo_r, tile_s, in_s,
):
    me = lax.axis_index("rows")
    rep = lax.axis_index("rep")
    other = 1 - rep
    mz, mp = me // ps, me % ps
    half, f_in = feat.shape

    paired = zs & (zs - 1) == 0

    def zto(k):
        return flip(mz, k) if paired else (mz + k) % zs

    def zfrom(k):
        return flip(mz, k) if paired else (mz + zs - k) % zs

    def prow(d):
        return (mp + d) % ps

    def send(src, dst, ssem, rsem, row, core):
        copy = pltpu.make_async_remote_copy(
            src_ref=src, dst_ref=dst, send_sem=ssem, recv_sem=rsem,
            device_id=(row, core), device_id_type=MESH,
        )
        copy.start()
        sent.append(copy)
        return copy

    def arrived(dst, ssem, rsem):
        pltpu.make_async_remote_copy(
            src_ref=dst, dst_ref=dst, send_sem=ssem, recv_sem=rsem,
            device_id=(me, other), device_id_type=MESH,
        ).wait_recv()

    sent = []
    tiles = counts.shape[0]
    parts = tile_s.shape[0]
    size = half // parts
    loads = []
    for k, (src, dst) in enumerate((
        (feat_h, feat), (rows_h, rows_v), (cols_h, cols_v), (ids_h, ids), (cot_h, cot),
        (ws_h, ws), (wn_h, wn),
    )):
        loads.append(pltpu.make_async_copy(src, dst, in_s.at[k]))
        loads[-1].start()

    def part_copy(c):
        span_i = pl.ds(pl.multiple_of(c * size, size), size)
        return pltpu.make_async_copy(counts.at[:, span_i], buf.at[:, span_i], tile_s.at[c])

    barrier = pltpu.get_barrier_semaphore()
    for d in range(1, zs):
        pl.semaphore_signal(barrier, inc=1, device_id=(zto(d) * ps + mp, rep), device_id_type=MESH)
    for d in range(1, ps):
        for core in (rep, other):
            pl.semaphore_signal(
                barrier, inc=1, device_id=(mz * ps + prow(d), core), device_id_type=MESH
            )
    pl.semaphore_signal(barrier, inc=1, device_id=(me, other), device_id_type=MESH)
    loads[0].wait()
    for c in range(parts):
        part_copy(c).start()
    pl.semaphore_wait(barrier, zs + 2 * (ps - 1))

    for d in range(1, zs):
        send(feat, gath.at[me], ag_s.at[d - 1], ag_r.at[me], zto(d) * ps + mp, rep)
    for d in range(1, ps):
        send(feat, gath.at[me], ag_s.at[zs - 2 + d], ag_r.at[me], mz * ps + prow(d), rep)
    for load in loads[1:]:
        load.wait()

    wide = pick.shape[1]
    sub = wide // tiles
    lane = lax.broadcasted_iota(jnp.int32, (tiles, wide), 1)
    widen = (lane // sub == lax.broadcasted_iota(jnp.int32, (tiles, wide), 0)).astype(jnp.float32)
    both = jnp.concatenate(
        [
            jnp.broadcast_to(rows_v[...], (8, tiles)),
            jnp.broadcast_to(cols_v[...] // 2, (8, tiles)),
        ],
        axis=0,
    ).astype(jnp.float32).astype(jnp.bfloat16)
    spread = dot(both, widen.astype(jnp.bfloat16)).astype(jnp.int32)
    place = (spread[:1] * n + spread[8:9]) * sub + lane[:1] % sub
    chunk = min(pick.shape[0], 2 * half)

    def pick_rows(b):
        at = lax.broadcasted_iota(jnp.int32, (chunk, wide), 0) + b * chunk
        pick[pl.ds(b * chunk, chunk), :] = (at == place).astype(jnp.float32).astype(jnp.bfloat16)

    def build(g):
        lows, highs = [
            buf[:, pl.ds(pl.multiple_of(g * size + k * sub, sub), sub), :]
            .astype(jnp.float32).reshape(wide, half).astype(jnp.bfloat16)
            for k in range(2)
        ]
        rhs = jnp.concatenate([lows, highs], axis=1)

        def fill(b):
            out = dot(pick[pl.ds(b * chunk, chunk), :], rhs)
            for k in range(chunk // sub):
                cell = b * (chunk // sub) + k
                pair = out[k * sub : (k + 1) * sub]
                adj[
                    pl.ds(pl.multiple_of(cell // n * half + g * size, size), size),
                    pl.ds(pl.multiple_of(cell % n * half, half), half),
                ] = jnp.concatenate([pair[:, :half], pair[:, half:]], axis=0).astype(jnp.bfloat16)

        blocks = pick.shape[0] // chunk
        if blocks == 1:
            fill(0)
        else:
            pl.loop(0, blocks)(fill)

    for b in range(pick.shape[0] // chunk):
        pick_rows(b)
    gath[me] = feat[...]
    first = dot(feat[...], ws[...])
    near = lax.broadcasted_iota(jnp.int32, (half, ids.shape[1]), 0)
    hits = (near == ids[...] - (me * 2 + rep) * half).astype(jnp.float32)
    masked = cot[...].astype(jnp.float32) * jnp.max(hits, axis=1, keepdims=True)

    def pass_on(e):
        src = zfrom(e) * ps + mp
        arrived(gath.at[src], ag_s.at[0], ag_r.at[src])
        for d in range(1, ps):
            send(
                gath.at[src], gath.at[src], ag_s.at[zs - 2 + e * (ps - 1) + d], ag_r.at[src],
                mz * ps + prow(d), rep,
            )

    def build_next(g):
        part_copy(g).wait()
        build(g)

    lead = parts // 2
    pl.loop(0, lead)(build_next)
    for e in range(1, zs):
        pass_on(e)
        if lead < parts:
            build_next(lead)
            lead += 1
    if lead < parts:
        pl.loop(lead, parts)(build_next)

    span = ps * half

    def plane_cols(zt):
        return adj[:, pl.ds(pl.multiple_of(zt * span, span), span)]

    total = jnp.zeros((2 * half, f_in), jnp.float32)
    for e in range(zs):
        zt = zfrom(e)
        for d in range(1, ps):
            src = zt * ps + prow(ps - d)
            arrived(gath.at[src], ag_s.at[0], ag_r.at[src])
        total = total + dot(plane_cols(zt), gath[pl.ds(zt * ps, ps)].reshape(span, f_in))
    part[...] = total.reshape(2, half, f_in)
    send(part.at[other], part_in, pair_s.at[0], pair_r.at[0], me, other)
    arrived(part_in, pair_s.at[0], pair_r.at[0])
    neighbour = (scale * (part[rep] + part_in[...])).astype(jnp.bfloat16)
    preact = first + dot(neighbour, wn[...])
    sigma = jax.nn.sigmoid(preact)
    delta = (masked * sigma * (1.0 + preact * (1.0 - sigma))).astype(jnp.bfloat16)
    bt[rep] = dot(wn[...], delta, NT).astype(jnp.bfloat16)
    send(bt.at[rep], bt.at[rep], pair_s.at[1], pair_r.at[1], me, other)
    wpart[0] = dot(feat[...], delta, TN).astype(jnp.bfloat16).reshape(wpart.shape[1:])
    wpart[1] = dot(neighbour, delta, TN).astype(jnp.bfloat16).reshape(wpart.shape[1:])
    peers = [(mp, other)] + [(prow(d), core) for d in range(1, ps) for core in (rep, other)]
    for k, (p, core) in enumerate(peers):
        send(
            wpart.at[core, p], win.at[rep, mp], w1_s.at[k], w1_r.at[rep, mp], mz * ps + p, core
        )
    act_out[...] = (preact * sigma).astype(jnp.bfloat16)
    own_term = dot(delta, ws[...], NT)

    arrived(bt.at[other], pair_s.at[1], pair_r.at[1])
    back = jnp.concatenate([bt[0], bt[1]], axis=1)

    def products(e):
        zt = zto(e)
        out = dot(back, plane_cols(zt))
        for j in range(ps):
            tt[zt * ps + j] = out[:, j * half : (j + 1) * half].astype(jnp.bfloat16)
        for d in range(1, ps):
            k = zt * (ps - 1) + d - 1
            send(
                tt.at[zt * ps + prow(d)], r1.at[k], r1_s.at[e * (ps - 1) + d - 1],
                r1_r.at[k], mz * ps + prow(d), rep,
            )

    for e in range(zs - 1, -1, -1):
        products(e)
    shard = wpart[rep, mp].astype(jnp.float32)
    for p, core in peers:
        arrived(win.at[core, p], w1_s.at[0], w1_r.at[core, p])
        shard = shard + win[core, p].astype(jnp.float32)
    wz[mz] = shard.astype(jnp.bfloat16)
    for d in range(1, zs):
        send(wz.at[mz], wz.at[mz], wz_s.at[d - 1], wz_r.at[mz], zto(d) * ps + mp, rep)

    def plane_sum(zt):
        total = tt[zt * ps + mp].astype(jnp.float32)
        for d in range(1, ps):
            k = zt * (ps - 1) + d - 1
            arrived(r1.at[k], r1_s.at[0], r1_r.at[k])
            total = total + r1[k].astype(jnp.float32)
        return total

    def spread_weights():
        for d in range(1, zs):
            src = zfrom(d)
            arrived(wz.at[src], wz_s.at[0], wz_r.at[src])
        shard = wz[0].astype(jnp.float32)
        for k in range(1, zs):
            shard = shard + wz[k].astype(jnp.float32)
        wo[rep, mp] = (grad_scale * shard).astype(jnp.bfloat16)
        for k, (p, core) in enumerate(peers[1:] + peers[:1]):
            send(
                wo.at[rep, mp], wo.at[rep, mp], wo_s.at[k], wo_r.at[rep, mp], mz * ps + p, core
            )

    for e in range(zs - 1, 0, -1):
        s2[e - 1] = plane_sum(zto(e)).astype(jnp.bfloat16)
        send(s2.at[e - 1], r2.at[e - 1], r2_s.at[e - 1], r2_r.at[e - 1], zto(e) * ps + mp, rep)
        if e == max(zs - 2, 1):
            spread_weights()
    if zs == 1:
        spread_weights()
    total = plane_sum(mz)
    for e in range(1, zs):
        arrived(r2.at[e - 1], r2_s.at[0], r2_r.at[e - 1])
        total = total + r2[e - 1].astype(jnp.float32)
    grad_out[...] = own_term + scale * jnp.transpose(total)
    for p, core in peers:
        arrived(wo.at[core, p], wo_s.at[0], wo_r.at[core, p])
    self_out[...] = wo[0].astype(jnp.float32).reshape(self_out.shape)
    neigh_out[...] = wo[1].astype(jnp.float32).reshape(neigh_out.shape)
    for copy in sent:
        copy.wait_send()


def plane_size(n, width):
    return max(d for d in range(1, n + 1) if n % d == 0 and d * d <= 2 * n and width % (8 * d) == 0)


def shards(
    features, tile_counts, tile_row, tile_col, label_ids, cotangent, self_weight, neigh_weight
):
    half, f_in = features.shape
    hid = cotangent.shape[1]
    tile_total, block, _ = tile_counts.shape
    rep_count = lax.axis_size("rep")
    n = lax.axis_size("rows")
    per_half = half // block
    row_blocks = rep_count * per_half
    scale = (edge_moment * tile_total * rep_count * block / row_blocks) ** (-0.5)
    grad_scale = float(label_ids.shape[0] * n * rep_count) ** (-0.5)
    parts = half // 16
    sub = 8
    ps = plane_size(n, f_in)
    zs = n // ps
    bf, f4 = jnp.bfloat16, jnp.float32
    dma = pltpu.SemaphoreType.DMA
    vmem = pl.BlockSpec(memory_space=pltpu.VMEM)
    outs = pl.pallas_call(
        functools.partial(layer_kernel, n, zs, ps, scale, grad_scale),
        out_shape=(
            jax.ShapeDtypeStruct((half, hid), bf),
            jax.ShapeDtypeStruct((half, f_in), f4),
            jax.ShapeDtypeStruct((f_in, hid), f4),
            jax.ShapeDtypeStruct((f_in, hid), f4),
        ),
        in_specs=[pl.BlockSpec(memory_space=pltpu.HBM)] * 8,
        out_specs=(vmem,) * 4,
        scratch_shapes=[
            pltpu.VMEM((1, tile_total), jnp.int32),
            pltpu.VMEM((1, tile_total), jnp.int32),
            pltpu.VMEM((half, f_in), bf),
            pltpu.VMEM((1, label_ids.shape[0]), jnp.int32),
            pltpu.VMEM((half, hid), bf),
            pltpu.VMEM((f_in, hid), bf),
            pltpu.VMEM((f_in, hid), bf),
            pltpu.VMEM((row_blocks * n * sub, tile_total * sub), bf),
            pltpu.VMEM((tile_total, block, block), jnp.int32),
            pltpu.VMEM((row_blocks * block, n * block), bf),
            pltpu.VMEM((n, half, f_in), bf),
            pltpu.VMEM((2, half, f_in), f4),
            pltpu.VMEM((half, f_in), f4),
            pltpu.VMEM((2, f_in, half), bf),
            pltpu.VMEM((n, f_in, half), bf),
            pltpu.VMEM((zs * (ps - 1), f_in, half), bf),
            pltpu.VMEM((zs - 1, f_in, half), bf),
            pltpu.VMEM((zs - 1, f_in, half), bf),
            pltpu.VMEM((2, ps, f_in // ps, hid), bf),
            pltpu.VMEM((2, ps, f_in // ps, hid), bf),
            pltpu.VMEM((zs, f_in // ps, hid), bf),
            pltpu.VMEM((2, ps, f_in // ps, hid), bf),
            dma((n,)), dma((n,)), dma((2,)), dma((2,)),
            dma((zs * (ps - 1),)), dma((zs * (ps - 1),)), dma((zs - 1,)), dma((zs - 1,)),
            dma((2 * ps - 1,)), dma((2, ps)), dma((zs - 1,)), dma((zs,)),
            dma((2 * ps - 1,)), dma((2, ps)), dma((parts,)), dma((7,)),
        ],
        compiler_params=pltpu.CompilerParams(
            collective_id=0, has_side_effects=True, vmem_limit_bytes=50 * 1024 * 1024
        ),
        name="layer",
    )(*[
        pltpu.with_memory_space_constraint(a, pltpu.HBM)
        for a in (
            tile_row.reshape(1, -1), tile_col.reshape(1, -1), tile_counts, features,
            label_ids.reshape(1, -1), cotangent, self_weight, neigh_weight,
        )
    ])
    return finish(outs)


def solution(mesh):
    placed = (
        P(("rows", "rep"), None),
        P(("rows", "rep"), None, None),
        P(("rows", "rep")),
        P(("rows", "rep")),
        P(("rows", "rep")),
        P(("rows", "rep"), None),
        P(),
        P(),
    )
    return jax.shard_map(
        shards,
        mesh=mesh,
        in_specs=placed,
        out_specs=(P(("rows", "rep"), None), P(("rows", "rep"), None), P(), P()),
        check_vma=False,
    )
```

```python
import functools

import jax
import jax.numpy as jnp
from jax import lax
from jax.experimental import pallas as pl
from jax.experimental.pallas import tpu as pltpu
from jax.sharding import PartitionSpec as P

edge_moment = 14.0 / 96.0
MESH = pl.DeviceIdType.MESH
NT = (((1,), (1,)), ((), ()))
TN = (((0,), (0,)), ((), ()))


def dot(a, b, dims=(((1,), (0,)), ((), ()))):
    return lax.dot_general(a, b, dims, preferred_element_type=jnp.float32)


def finish_kernel(*refs):
    count = len(refs) // 2
    sems = refs[-1]
    copies = [
        pltpu.make_async_copy(refs[k], refs[count + k], sems.at[k]) for k in range(count)
    ]
    for copy in copies:
        copy.start()
    for copy in copies:
        copy.wait()


def finish(arrays):
    return pl.pallas_call(
        finish_kernel,
        out_shape=tuple(jax.ShapeDtypeStruct(a.shape, a.dtype) for a in arrays),
        in_specs=[pl.BlockSpec(memory_space=pltpu.VMEM)] * len(arrays),
        out_specs=tuple(pl.BlockSpec(memory_space=pl.ANY) for _ in arrays),
        scratch_shapes=[pltpu.SemaphoreType.DMA((len(arrays),))],
        compiler_params=pltpu.CompilerParams(vmem_limit_bytes=4 * 1024 * 1024),
        name="finish",
    )(*arrays)


def flip(a, k):
    out, bit = a, 1
    while bit <= k:
        if k & bit:
            out = out + (1 - 2 * ((a // bit) % 2)) * bit
        bit *= 2
    return out


def layer_kernel(
    n, zs, ps, scale, grad_scale,
    rows_h, cols_h, counts, feat_h, ids_h, cot_h, ws_h, wn_h,
    act_out, grad_out, self_out, neigh_out,
    rows_v, cols_v, feat, ids, cot, ws, wn, pick, buf, adj, gath, part, part_in, bt, tt, r1, s2, r2, wpart, win, wz, wo,
    send_s, ag_z, ag_r, pair_r, r1_r, late_r, tile_s, in_s,
):
    me = lax.axis_index("rows")
    rep = lax.axis_index("rep")
    other = 1 - rep
    mz, mp = me // ps, me % ps
    half, f_in = feat.shape

    paired = zs & (zs - 1) == 0

    def zto(k):
        return flip(mz, k) if paired else (mz + k) % zs

    def zfrom(k):
        return flip(mz, k) if paired else (mz + zs - k) % zs

    def prow(d):
        return (mp + d) % ps

    def send(src, dst, ssem, rsem, row, core):
        copy = pltpu.make_async_remote_copy(
            src_ref=src, dst_ref=dst, send_sem=ssem, recv_sem=rsem,
            device_id=(row, core), device_id_type=MESH,
        )
        copy.start()

    def whole(ref, ssem, rsem):
        return pltpu.make_async_remote_copy(
            src_ref=ref, dst_ref=ref, send_sem=ssem, recv_sem=rsem,
            device_id=(me, other), device_id_type=MESH,
        )

    def arrived(dst, rsem):
        whole(dst, rsem, rsem).wait_recv()

    def left(src, ssem):
        whole(src, ssem, ssem).wait_send()

    tiles = counts.shape[0]
    parts = tile_s.shape[0]
    size = half // parts
    loads = []
    for k, (src, dst) in enumerate((
        (feat_h, feat), (rows_h, rows_v), (cols_h, cols_v), (ids_h, ids), (cot_h, cot),
        (ws_h, ws), (wn_h, wn),
    )):
        loads.append(pltpu.make_async_copy(src, dst, in_s.at[k]))
        loads[-1].start()

    def part_copy(c):
        span_i = pl.ds(pl.multiple_of(c * size, size), size)
        return pltpu.make_async_copy(counts.at[:, span_i], buf.at[:, span_i], tile_s.at[c])

    barrier = pltpu.get_barrier_semaphore()
    for d in range(1, zs):
        pl.semaphore_signal(barrier, inc=1, device_id=(zto(d) * ps + mp, rep), device_id_type=MESH)
    for d in range(1, ps):
        for core in (rep, other):
            pl.semaphore_signal(
                barrier, inc=1, device_id=(mz * ps + prow(d), core), device_id_type=MESH
            )
    pl.semaphore_signal(barrier, inc=1, device_id=(me, other), device_id_type=MESH)
    cube = range(1, ps) if zs > 1 else ()
    for d in cube:
        pl.semaphore_signal(
            barrier, inc=1, device_id=(zto(1) * ps + prow(d), rep), device_id_type=MESH
        )
    loads[0].wait()
    for c in range(parts):
        part_copy(c).start()
    pl.semaphore_wait(barrier, zs + 2 * (ps - 1) + len(cube))

    firsts = [zto(k) * ps + mp for k in [*range(2, zs), 1] if k < zs]
    firsts += [mz * ps + prow(d) for d in range(1, ps)]
    firsts += [zto(1) * ps + prow(d) for d in cube]
    relayed = max(zs - 2, 0)
    for k, row in enumerate(firsts):
        rsem = ag_z.at[mz] if k < relayed else ag_r.at[mz]
        send(feat, gath.at[me], send_s.at[0], rsem, row, rep)
    for load in loads[1:]:
        load.wait()

    wide = pick.shape[1]
    sub = wide // tiles
    lane = lax.broadcasted_iota(jnp.int32, (tiles, wide), 1)
    widen = (lane // sub == lax.broadcasted_iota(jnp.int32, (tiles, wide), 0)).astype(jnp.float32)
    both = jnp.concatenate(
        [
            jnp.broadcast_to(rows_v[...], (8, tiles)),
            jnp.broadcast_to(cols_v[...] // 2, (8, tiles)),
        ],
        axis=0,
    ).astype(jnp.float32).astype(jnp.bfloat16)
    spread = dot(both, widen.astype(jnp.bfloat16)).astype(jnp.int32)
    place = (spread[:1] * n + spread[8:9]) * sub + lane[:1] % sub
    chunk = min(pick.shape[0], 2 * half)

    def pick_rows(b):
        at = lax.broadcasted_iota(jnp.int32, (chunk, wide), 0) + b * chunk
        pick[pl.ds(b * chunk, chunk), :] = (at == place).astype(jnp.float32).astype(jnp.bfloat16)

    def build(g):
        lows, highs = [
            buf[:, pl.ds(pl.multiple_of(g * size + k * sub, sub), sub), :]
            .astype(jnp.float32).reshape(wide, half).astype(jnp.bfloat16)
            for k in range(2)
        ]
        rhs = jnp.concatenate([lows, highs], axis=1)

        def fill(b):
            out = dot(pick[pl.ds(b * chunk, chunk), :], rhs)
            for k in range(chunk // sub):
                cell = b * (chunk // sub) + k
                pair = out[k * sub : (k + 1) * sub]
                adj[
                    pl.ds(pl.multiple_of(cell // n * half + g * size, size), size),
                    pl.ds(pl.multiple_of(cell % n * half, half), half),
                ] = jnp.concatenate([pair[:, :half], pair[:, half:]], axis=0).astype(jnp.bfloat16)

        blocks = pick.shape[0] // chunk
        if blocks == 1:
            fill(0)
        else:
            pl.loop(0, blocks)(fill)

    for b in range(pick.shape[0] // chunk):
        pick_rows(b)
    gath[me] = feat[...]
    first = dot(feat[...], ws[...])
    near = lax.broadcasted_iota(jnp.int32, (half, ids.shape[1]), 0)
    hits = (near == ids[...] - (me * 2 + rep) * half).astype(jnp.float32)
    masked = cot[...].astype(jnp.float32) * jnp.max(hits, axis=1, keepdims=True)

    def pass_on(e):
        src = zfrom(e) * ps + mp
        arrived(gath.at[src], ag_z.at[zfrom(e)])
        for d in range(1, ps):
            send(
                gath.at[src], gath.at[src], send_s.at[0], ag_r.at[zfrom(e)],
                mz * ps + prow(d), rep,
            )

    def build_next(g):
        part_copy(g).wait()
        build(g)

    lead = parts // 2
    pl.loop(0, lead)(build_next)
    for e in range(2, zs):
        pass_on(e)
        if lead < parts:
            build_next(lead)
            lead += 1
    if lead < parts:
        pl.loop(lead, parts)(build_next)

    span = ps * half

    def plane_cols(zt):
        return adj[:, pl.ds(pl.multiple_of(zt * span, span), span)]

    total = jnp.zeros((2 * half, f_in), jnp.float32)
    for e in range(zs):
        zt = zfrom(e)
        landing = ps if e == 1 else ps - 1
        if landing:
            arrived(gath.at[pl.ds(zt * ps, landing)], ag_r.at[zt])
        total = total + dot(plane_cols(zt), gath[pl.ds(zt * ps, ps)].reshape(span, f_in))
    part[...] = total.reshape(2, half, f_in)
    send(part.at[other], part_in, send_s.at[1], pair_r.at[0], me, other)
    arrived(part_in, pair_r.at[0])
    neighbour = (scale * (part[rep] + part_in[...])).astype(jnp.bfloat16)
    preact = first + dot(neighbour, wn[...])
    sigma = jax.nn.sigmoid(preact)
    delta = (masked * sigma * (1.0 + preact * (1.0 - sigma))).astype(jnp.bfloat16)
    bt[rep] = dot(wn[...], delta, NT).astype(jnp.bfloat16)
    send(bt.at[rep], bt.at[rep], send_s.at[2], pair_r.at[1], me, other)
    wpart[0] = dot(feat[...], delta, TN).astype(jnp.bfloat16).reshape(wpart.shape[1:])
    wpart[1] = dot(neighbour, delta, TN).astype(jnp.bfloat16).reshape(wpart.shape[1:])
    peers = [(mp, other)] + [(prow(d), core) for d in range(1, ps) for core in (rep, other)]
    for p, core in peers:
        send(
            wpart.at[core, p], win.at[rep * ps + mp], send_s.at[3], late_r.at[0], mz * ps + p, core
        )
    act_out[...] = (preact * sigma).astype(jnp.bfloat16)
    own_term = dot(delta, ws[...], NT)

    arrived(bt.at[other], pair_r.at[1])
    back = jnp.concatenate([bt[0], bt[1]], axis=1)

    def products(e):
        zt = zto(e)
        out = dot(back, plane_cols(zt))
        for j in range(ps):
            tt[zt * ps + j] = out[:, j * half : (j + 1) * half].astype(jnp.bfloat16)
        for d in range(1, ps):
            k = zt * (ps - 1) + d - 1
            send(
                tt.at[zt * ps + prow(d)], r1.at[k], send_s.at[4],
                r1_r.at[zt], mz * ps + prow(d), rep,
            )

    for e in range(zs - 1, -1, -1):
        products(e)
    shard = wpart[rep, mp].astype(jnp.float32)
    arrived(win.at[pl.ds(0, len(peers))], late_r.at[0])
    for p, core in peers:
        shard = shard + win[core * ps + p].astype(jnp.float32)
    wz[mz] = shard.astype(jnp.bfloat16)
    for d in range(1, zs):
        send(wz.at[mz], wz.at[mz], send_s.at[5], late_r.at[1], zto(d) * ps + mp, rep)

    def plane_sum(zt):
        total = tt[zt * ps + mp].astype(jnp.float32)
        if ps > 1:
            arrived(r1.at[pl.ds(zt * (ps - 1), ps - 1)], r1_r.at[zt])
        for d in range(1, ps):
            k = zt * (ps - 1) + d - 1
            total = total + r1[k].astype(jnp.float32)
        return total

    def spread_weights():
        if zs > 1:
            arrived(wz.at[pl.ds(0, zs - 1)], late_r.at[1])
        shard = wz[0].astype(jnp.float32)
        for k in range(1, zs):
            shard = shard + wz[k].astype(jnp.float32)
        mine = rep * ps + mp
        wo[mine] = (grad_scale * shard).astype(jnp.bfloat16)
        for p, core in peers[1:] + peers[:1]:
            send(wo.at[mine], wo.at[mine], send_s.at[6], late_r.at[2], mz * ps + p, core)

    for e in range(zs - 1, 0, -1):
        s2[e - 1] = plane_sum(zto(e)).astype(jnp.bfloat16)
        send(s2.at[e - 1], r2.at[e - 1], send_s.at[7], late_r.at[3], zto(e) * ps + mp, rep)
        if e == max(zs - 2, 1):
            spread_weights()
    if zs == 1:
        spread_weights()
    total = plane_sum(mz)
    if zs > 1:
        arrived(r2, late_r.at[3])
    for e in range(1, zs):
        total = total + r2[e - 1].astype(jnp.float32)
    grad_out[...] = own_term + scale * jnp.transpose(total)
    arrived(wo.at[pl.ds(0, len(peers))], late_r.at[2])
    self_out[...] = wo[:ps].astype(jnp.float32).reshape(self_out.shape)
    neigh_out[...] = wo[ps:].astype(jnp.float32).reshape(neigh_out.shape)
    if n > 1:
        left(gath.at[pl.ds(0, n - 1)], send_s.at[0])
    left(part_in, send_s.at[1])
    left(bt.at[rep], send_s.at[2])
    left(win.at[pl.ds(0, len(peers))], send_s.at[3])
    if ps > 1:
        left(r1, send_s.at[4])
    if zs > 1:
        left(wz.at[pl.ds(0, zs - 1)], send_s.at[5])
        left(r2, send_s.at[7])
    left(wo.at[pl.ds(0, len(peers))], send_s.at[6])


def plane_size(n, width):
    return max(d for d in range(1, n + 1) if n % d == 0 and d * d <= 2 * n and width % (8 * d) == 0)


def shards(
    features, tile_counts, tile_row, tile_col, label_ids, cotangent, self_weight, neigh_weight
):
    half, f_in = features.shape
    hid = cotangent.shape[1]
    tile_total, block, _ = tile_counts.shape
    rep_count = lax.axis_size("rep")
    n = lax.axis_size("rows")
    per_half = half // block
    row_blocks = rep_count * per_half
    scale = (edge_moment * tile_total * rep_count * block / row_blocks) ** (-0.5)
    grad_scale = float(label_ids.shape[0] * n * rep_count) ** (-0.5)
    parts = half // 16
    sub = 8
    ps = plane_size(n, f_in)
    zs = n // ps
    bf, f4 = jnp.bfloat16, jnp.float32
    dma = pltpu.SemaphoreType.DMA
    vmem = pl.BlockSpec(memory_space=pltpu.VMEM)
    outs = pl.pallas_call(
        functools.partial(layer_kernel, n, zs, ps, scale, grad_scale),
        out_shape=(
            jax.ShapeDtypeStruct((half, hid), bf),
            jax.ShapeDtypeStruct((half, f_in), f4),
            jax.ShapeDtypeStruct((f_in, hid), f4),
            jax.ShapeDtypeStruct((f_in, hid), f4),
        ),
        in_specs=[pl.BlockSpec(memory_space=pltpu.HBM)] * 8,
        out_specs=(vmem,) * 4,
        scratch_shapes=[
            pltpu.VMEM((1, tile_total), jnp.int32),
            pltpu.VMEM((1, tile_total), jnp.int32),
            pltpu.VMEM((half, f_in), bf),
            pltpu.VMEM((1, label_ids.shape[0]), jnp.int32),
            pltpu.VMEM((half, hid), bf),
            pltpu.VMEM((f_in, hid), bf),
            pltpu.VMEM((f_in, hid), bf),
            pltpu.VMEM((row_blocks * n * sub, tile_total * sub), bf),
            pltpu.VMEM((tile_total, block, block), jnp.int32),
            pltpu.VMEM((row_blocks * block, n * block), bf),
            pltpu.VMEM((n, half, f_in), bf),
            pltpu.VMEM((2, half, f_in), f4),
            pltpu.VMEM((half, f_in), f4),
            pltpu.VMEM((2, f_in, half), bf),
            pltpu.VMEM((n, f_in, half), bf),
            pltpu.VMEM((zs * (ps - 1), f_in, half), bf),
            pltpu.VMEM((zs - 1, f_in, half), bf),
            pltpu.VMEM((zs - 1, f_in, half), bf),
            pltpu.VMEM((2, ps, f_in // ps, hid), bf),
            pltpu.VMEM((2 * ps, f_in // ps, hid), bf),
            pltpu.VMEM((zs, f_in // ps, hid), bf),
            pltpu.VMEM((2 * ps, f_in // ps, hid), bf),
            dma((8,)), dma((zs,)), dma((zs,)), dma((2,)), dma((zs,)), dma((4,)), dma((parts,)),
            dma((7,)),
        ],
        compiler_params=pltpu.CompilerParams(
            collective_id=0, has_side_effects=True, vmem_limit_bytes=50 * 1024 * 1024
        ),
        name="layer",
    )(*[
        pltpu.with_memory_space_constraint(a, pltpu.HBM)
        for a in (
            tile_row.reshape(1, -1), tile_col.reshape(1, -1), tile_counts, features,
            label_ids.reshape(1, -1), cotangent, self_weight, neigh_weight,
        )
    ])
    return finish(outs)


def solution(mesh):
    placed = (
        P(("rows", "rep"), None),
        P(("rows", "rep"), None, None),
        P(("rows", "rep")),
        P(("rows", "rep")),
        P(("rows", "rep")),
        P(("rows", "rep"), None),
        P(),
        P(),
    )
    return jax.shard_map(
        shards,
        mesh=mesh,
        in_specs=placed,
        out_specs=(P(("rows", "rep"), None), P(("rows", "rep"), None), P(), P()),
        check_vma=False,
    )
```

```python
import functools

import jax
import jax.numpy as jnp
from jax import lax
from jax.experimental import pallas as pl
from jax.experimental.pallas import tpu as pltpu
from jax.sharding import PartitionSpec as P

edge_moment = 14.0 / 96.0
MESH = pl.DeviceIdType.MESH
NT = (((1,), (1,)), ((), ()))
TN = (((0,), (0,)), ((), ()))


def dot(a, b, dims=(((1,), (0,)), ((), ()))):
    return lax.dot_general(a, b, dims, preferred_element_type=jnp.float32)


def finish_kernel(*refs):
    count = len(refs) // 2
    sems = refs[-1]
    copies = [
        pltpu.make_async_copy(refs[k], refs[count + k], sems.at[k]) for k in range(count)
    ]
    for copy in copies:
        copy.start()
    for copy in copies:
        copy.wait()


def finish(arrays):
    return pl.pallas_call(
        finish_kernel,
        out_shape=tuple(jax.ShapeDtypeStruct(a.shape, a.dtype) for a in arrays),
        in_specs=[pl.BlockSpec(memory_space=pltpu.VMEM)] * len(arrays),
        out_specs=tuple(pl.BlockSpec(memory_space=pl.ANY) for _ in arrays),
        scratch_shapes=[pltpu.SemaphoreType.DMA((len(arrays),))],
        compiler_params=pltpu.CompilerParams(vmem_limit_bytes=4 * 1024 * 1024),
        name="finish",
    )(*arrays)


def flip(a, k):
    out, bit = a, 1
    while bit <= k:
        if k & bit:
            out = out + (1 - 2 * ((a // bit) % 2)) * bit
        bit *= 2
    return out


def layer_kernel(
    n, zs, ps, scale, grad_scale,
    rows_h, cols_h, counts, feat_h, ids_h, cot_h, ws_h, wn_h,
    act_out, grad_out, self_out, neigh_out,
    rows_v, cols_v, feat, ids, cot, ws, wn, pick, buf, adj, gath, part, part_in, bt, tt, r1, s2, r2, wpart, win, wz, wo,
    send_s, ag_z, ag_r, pair_r, r1_r, late_r, tile_s, in_s,
):
    me = lax.axis_index("rows")
    rep = lax.axis_index("rep")
    other = 1 - rep
    mz, mp = me // ps, me % ps
    half, f_in = feat.shape

    paired = zs & (zs - 1) == 0

    def zto(k):
        return flip(mz, k) if paired else (mz + k) % zs

    def zfrom(k):
        return flip(mz, k) if paired else (mz + zs - k) % zs

    def prow(d):
        return flip(mp, d) if ps & (ps - 1) == 0 else (mp + d) % ps

    outer = range(ps - 1, 0, -1)

    def send(src, dst, ssem, rsem, row, core):
        copy = pltpu.make_async_remote_copy(
            src_ref=src, dst_ref=dst, send_sem=ssem, recv_sem=rsem,
            device_id=(row, core), device_id_type=MESH,
        )
        copy.start()

    def whole(ref, ssem, rsem):
        return pltpu.make_async_remote_copy(
            src_ref=ref, dst_ref=ref, send_sem=ssem, recv_sem=rsem,
            device_id=(me, other), device_id_type=MESH,
        )

    def arrived(dst, rsem):
        whole(dst, rsem, rsem).wait_recv()

    def left(src, ssem):
        whole(src, ssem, ssem).wait_send()

    tiles = counts.shape[0]
    parts = tile_s.shape[0]
    size = half // parts
    loads = []
    for k, (src, dst) in enumerate((
        (feat_h, feat), (rows_h, rows_v), (cols_h, cols_v), (ids_h, ids), (cot_h, cot),
        (ws_h, ws), (wn_h, wn),
    )):
        loads.append(pltpu.make_async_copy(src, dst, in_s.at[k]))
        loads[-1].start()

    def part_copy(c):
        span_i = pl.ds(pl.multiple_of(c * size, size), size)
        return pltpu.make_async_copy(counts.at[:, span_i], buf.at[:, span_i], tile_s.at[c])

    barrier = pltpu.get_barrier_semaphore()
    for d in range(1, zs):
        pl.semaphore_signal(barrier, inc=1, device_id=(zto(d) * ps + mp, rep), device_id_type=MESH)
    for d in range(1, ps):
        for core in (rep, other):
            pl.semaphore_signal(
                barrier, inc=1, device_id=(mz * ps + prow(d), core), device_id_type=MESH
            )
    pl.semaphore_signal(barrier, inc=1, device_id=(me, other), device_id_type=MESH)
    cube = outer if zs > 1 else ()
    for d in cube:
        pl.semaphore_signal(
            barrier, inc=1, device_id=(zto(1) * ps + prow(d), rep), device_id_type=MESH
        )
    loads[0].wait()
    for c in range(parts):
        part_copy(c).start()
    pl.semaphore_wait(barrier, zs + 2 * (ps - 1) + len(cube))

    firsts = [zto(k) * ps + mp for k in [*range(2, zs), 1] if k < zs]
    firsts += [mz * ps + prow(d) for d in outer]
    firsts += [zto(1) * ps + prow(d) for d in cube]
    relayed = max(zs - 2, 0)
    for k, row in enumerate(firsts):
        rsem = ag_z.at[mz] if k < relayed else ag_r.at[mz]
        send(feat, gath.at[me], send_s.at[0], rsem, row, rep)
    for load in loads[1:]:
        load.wait()

    wide = pick.shape[1]
    sub = wide // tiles
    lane = lax.broadcasted_iota(jnp.int32, (tiles, wide), 1)
    widen = (lane // sub == lax.broadcasted_iota(jnp.int32, (tiles, wide), 0)).astype(jnp.float32)
    both = jnp.concatenate(
        [
            jnp.broadcast_to(rows_v[...], (8, tiles)),
            jnp.broadcast_to(cols_v[...] // 2, (8, tiles)),
        ],
        axis=0,
    ).astype(jnp.float32).astype(jnp.bfloat16)
    spread = dot(both, widen.astype(jnp.bfloat16)).astype(jnp.int32)
    place = (spread[:1] * n + spread[8:9]) * sub + lane[:1] % sub
    chunk = min(pick.shape[0], 2 * half)

    def pick_rows(b):
        at = lax.broadcasted_iota(jnp.int32, (chunk, wide), 0) + b * chunk
        pick[pl.ds(b * chunk, chunk), :] = (at == place).astype(jnp.float32).astype(jnp.bfloat16)

    def build(g):
        lows, highs = [
            buf[:, pl.ds(pl.multiple_of(g * size + k * sub, sub), sub), :]
            .astype(jnp.float32).reshape(wide, half).astype(jnp.bfloat16)
            for k in range(2)
        ]
        rhs = jnp.concatenate([lows, highs], axis=1)

        def fill(b):
            out = dot(pick[pl.ds(b * chunk, chunk), :], rhs)
            for k in range(chunk // sub):
                cell = b * (chunk // sub) + k
                pair = out[k * sub : (k + 1) * sub]
                adj[
                    pl.ds(pl.multiple_of(cell // n * half + g * size, size), size),
                    pl.ds(pl.multiple_of(cell % n * half, half), half),
                ] = jnp.concatenate([pair[:, :half], pair[:, half:]], axis=0).astype(jnp.bfloat16)

        blocks = pick.shape[0] // chunk
        if blocks == 1:
            fill(0)
        else:
            pl.loop(0, blocks)(fill)

    for b in range(pick.shape[0] // chunk):
        pick_rows(b)
    gath[me] = feat[...]
    first = dot(feat[...], ws[...])
    near = lax.broadcasted_iota(jnp.int32, (half, ids.shape[1]), 0)
    hits = (near == ids[...] - (me * 2 + rep) * half).astype(jnp.float32)
    masked = cot[...].astype(jnp.float32) * jnp.max(hits, axis=1, keepdims=True)

    def pass_on(e):
        src = zfrom(e) * ps + mp
        arrived(gath.at[src], ag_z.at[zfrom(e)])
        for d in outer:
            send(
                gath.at[src], gath.at[src], send_s.at[0], ag_r.at[zfrom(e)],
                mz * ps + prow(d), rep,
            )

    def build_next(g):
        part_copy(g).wait()
        build(g)

    lead = parts // 2
    pl.loop(0, lead)(build_next)
    for e in range(2, zs):
        pass_on(e)
        if lead < parts:
            build_next(lead)
            lead += 1
    if lead < parts:
        pl.loop(lead, parts)(build_next)

    span = ps * half

    def plane_cols(zt):
        return adj[:, pl.ds(pl.multiple_of(zt * span, span), span)]

    total = jnp.zeros((2 * half, f_in), jnp.float32)
    for e in range(zs):
        zt = zfrom(e)
        landing = ps if e == 1 else ps - 1
        if landing:
            arrived(gath.at[pl.ds(zt * ps, landing)], ag_r.at[zt])
        total = total + dot(plane_cols(zt), gath[pl.ds(zt * ps, ps)].reshape(span, f_in))
    part[...] = total.reshape(2, half, f_in)
    send(part.at[other], part_in, send_s.at[1], pair_r.at[0], me, other)
    arrived(part_in, pair_r.at[0])
    neighbour = (scale * (part[rep] + part_in[...])).astype(jnp.bfloat16)
    preact = first + dot(neighbour, wn[...])
    sigma = jax.nn.sigmoid(preact)
    delta = (masked * sigma * (1.0 + preact * (1.0 - sigma))).astype(jnp.bfloat16)
    bt[rep] = dot(wn[...], delta, NT).astype(jnp.bfloat16)
    send(bt.at[rep], bt.at[rep], send_s.at[2], pair_r.at[1], me, other)
    wpart[0] = dot(feat[...], delta, TN).astype(jnp.bfloat16).reshape(wpart.shape[1:])
    wpart[1] = dot(neighbour, delta, TN).astype(jnp.bfloat16).reshape(wpart.shape[1:])
    peers = [(mp, other)] + [(prow(d), core) for d in outer for core in (rep, other)]
    for p, core in peers:
        send(
            wpart.at[core, p], win.at[rep * ps + mp], send_s.at[3], late_r.at[0], mz * ps + p, core
        )
    act_out[...] = (preact * sigma).astype(jnp.bfloat16)
    own_term = dot(delta, ws[...], NT)

    arrived(bt.at[other], pair_r.at[1])
    back = jnp.concatenate([bt[0], bt[1]], axis=1)

    def products(e):
        zt = zto(e)
        out = dot(back, plane_cols(zt))
        for j in range(ps):
            tt[zt * ps + j] = out[:, j * half : (j + 1) * half].astype(jnp.bfloat16)
        for d in outer:
            k = zt * (ps - 1) + d - 1
            send(
                tt.at[zt * ps + prow(d)], r1.at[k], send_s.at[4],
                r1_r.at[zt], mz * ps + prow(d), rep,
            )

    for e in range(zs - 1, -1, -1):
        products(e)
    shard = wpart[rep, mp].astype(jnp.float32)
    arrived(win.at[pl.ds(0, len(peers))], late_r.at[0])
    for p, core in peers:
        shard = shard + win[core * ps + p].astype(jnp.float32)
    wz[mz] = shard.astype(jnp.bfloat16)
    for d in range(zs - 1, 0, -1):
        send(wz.at[mz], wz.at[mz], send_s.at[5], late_r.at[1], zto(d) * ps + mp, rep)

    def plane_sum(zt):
        total = tt[zt * ps + mp].astype(jnp.float32)
        if ps > 1:
            arrived(r1.at[pl.ds(zt * (ps - 1), ps - 1)], r1_r.at[zt])
        for d in range(1, ps):
            k = zt * (ps - 1) + d - 1
            total = total + r1[k].astype(jnp.float32)
        return total

    def spread_weights():
        if zs > 1:
            arrived(wz.at[pl.ds(0, zs - 1)], late_r.at[1])
        shard = wz[0].astype(jnp.float32)
        for k in range(1, zs):
            shard = shard + wz[k].astype(jnp.float32)
        mine = rep * ps + mp
        wo[mine] = (grad_scale * shard).astype(jnp.bfloat16)
        for p, core in peers[1:] + peers[:1]:
            send(wo.at[mine], wo.at[mine], send_s.at[6], late_r.at[2], mz * ps + p, core)

    for e in range(zs - 1, 0, -1):
        s2[e - 1] = plane_sum(zto(e)).astype(jnp.bfloat16)
        send(s2.at[e - 1], r2.at[e - 1], send_s.at[7], late_r.at[3], zto(e) * ps + mp, rep)
        if e == max(zs - 2, 1):
            spread_weights()
    if zs == 1:
        spread_weights()
    total = plane_sum(mz)
    if zs > 1:
        arrived(r2, late_r.at[3])
    for e in range(1, zs):
        total = total + r2[e - 1].astype(jnp.float32)
    grad_out[...] = own_term + scale * jnp.transpose(total)
    arrived(wo.at[pl.ds(0, len(peers))], late_r.at[2])
    self_out[...] = wo[:ps].astype(jnp.float32).reshape(self_out.shape)
    neigh_out[...] = wo[ps:].astype(jnp.float32).reshape(neigh_out.shape)
    if n > 1:
        left(gath.at[pl.ds(0, n - 1)], send_s.at[0])
    left(part_in, send_s.at[1])
    left(bt.at[rep], send_s.at[2])
    left(win.at[pl.ds(0, len(peers))], send_s.at[3])
    if ps > 1:
        left(r1, send_s.at[4])
    if zs > 1:
        left(wz.at[pl.ds(0, zs - 1)], send_s.at[5])
        left(r2, send_s.at[7])
    left(wo.at[pl.ds(0, len(peers))], send_s.at[6])


def plane_size(n, width):
    return max(d for d in range(1, n + 1) if n % d == 0 and d * d <= 2 * n and width % (8 * d) == 0)


def shards(
    features, tile_counts, tile_row, tile_col, label_ids, cotangent, self_weight, neigh_weight
):
    half, f_in = features.shape
    hid = cotangent.shape[1]
    tile_total, block, _ = tile_counts.shape
    rep_count = lax.axis_size("rep")
    n = lax.axis_size("rows")
    per_half = half // block
    row_blocks = rep_count * per_half
    scale = (edge_moment * tile_total * rep_count * block / row_blocks) ** (-0.5)
    grad_scale = float(label_ids.shape[0] * n * rep_count) ** (-0.5)
    parts = half // 16
    sub = 8
    ps = plane_size(n, f_in)
    zs = n // ps
    bf, f4 = jnp.bfloat16, jnp.float32
    dma = pltpu.SemaphoreType.DMA
    vmem = pl.BlockSpec(memory_space=pltpu.VMEM)
    outs = pl.pallas_call(
        functools.partial(layer_kernel, n, zs, ps, scale, grad_scale),
        out_shape=(
            jax.ShapeDtypeStruct((half, hid), bf),
            jax.ShapeDtypeStruct((half, f_in), f4),
            jax.ShapeDtypeStruct((f_in, hid), f4),
            jax.ShapeDtypeStruct((f_in, hid), f4),
        ),
        in_specs=[pl.BlockSpec(memory_space=pltpu.HBM)] * 8,
        out_specs=(vmem,) * 4,
        scratch_shapes=[
            pltpu.VMEM((1, tile_total), jnp.int32),
            pltpu.VMEM((1, tile_total), jnp.int32),
            pltpu.VMEM((half, f_in), bf),
            pltpu.VMEM((1, label_ids.shape[0]), jnp.int32),
            pltpu.VMEM((half, hid), bf),
            pltpu.VMEM((f_in, hid), bf),
            pltpu.VMEM((f_in, hid), bf),
            pltpu.VMEM((row_blocks * n * sub, tile_total * sub), bf),
            pltpu.VMEM((tile_total, block, block), jnp.int32),
            pltpu.VMEM((row_blocks * block, n * block), bf),
            pltpu.VMEM((n, half, f_in), bf),
            pltpu.VMEM((2, half, f_in), f4),
            pltpu.VMEM((half, f_in), f4),
            pltpu.VMEM((2, f_in, half), bf),
            pltpu.VMEM((n, f_in, half), bf),
            pltpu.VMEM((zs * (ps - 1), f_in, half), bf),
            pltpu.VMEM((zs - 1, f_in, half), bf),
            pltpu.VMEM((zs - 1, f_in, half), bf),
            pltpu.VMEM((2, ps, f_in // ps, hid), bf),
            pltpu.VMEM((2 * ps, f_in // ps, hid), bf),
            pltpu.VMEM((zs, f_in // ps, hid), bf),
            pltpu.VMEM((2 * ps, f_in // ps, hid), bf),
            dma((8,)), dma((zs,)), dma((zs,)), dma((2,)), dma((zs,)), dma((4,)), dma((parts,)),
            dma((7,)),
        ],
        compiler_params=pltpu.CompilerParams(
            collective_id=0, has_side_effects=True, vmem_limit_bytes=50 * 1024 * 1024
        ),
        name="layer",
    )(*[
        pltpu.with_memory_space_constraint(a, pltpu.HBM)
        for a in (
            tile_row.reshape(1, -1), tile_col.reshape(1, -1), tile_counts, features,
            label_ids.reshape(1, -1), cotangent, self_weight, neigh_weight,
        )
    ])
    return finish(outs)


def solution(mesh):
    placed = (
        P(("rows", "rep"), None),
        P(("rows", "rep"), None, None),
        P(("rows", "rep")),
        P(("rows", "rep")),
        P(("rows", "rep")),
        P(("rows", "rep"), None),
        P(),
        P(),
    )
    return jax.shard_map(
        shards,
        mesh=mesh,
        in_specs=placed,
        out_specs=(P(("rows", "rep"), None), P(("rows", "rep"), None), P(), P()),
        check_vma=False,
    )
```
